512 devices in a mesh: chan: 64 (over z, x, core), win: 8 (over y).
Axes of the slice: x: 4, y: 8, z: 8, core: 2. Of those that a mesh axis runs over, the one named last changes fastest.
Arguments:
- records: bfloat16 [32, 32768, 512], P('win', 'chan'), may hold values from -6 to 6
- block_pairs: int32 [2048, 2], P('chan'), may hold values from 0 to 255, as said below
- lag_low: int32 [2048], P('chan'), may hold values from 0 to 31
- lag_high: int32 [2048], P('chan'), may hold values from 97 to 128
- slot_count: int32 [64], P('chan'), may hold values from 1 to 32, as said below
Outputs:
- stacks: float32 [2048, 128, 128], P(('chan', 'win'))
The draws below stay inside these ranges and needn't reach their ends.
Inputs may be any that keep to these rules, and one draw needn't show every extreme that they name: `block_pairs`: slot p belongs to owner p // 32; for owner o both blocks of each slot lie within o * 4 - 16 to o * 4 + 19, and the two blocks differ by at most 16. Slots of owner o at or after slot_count[o] are unused; some owner uses all 32.
All inputs are finite; a program needn't handle non-finite values.
Results may differ from the reference program's by a relative error of at most 0.0015.
Values may be sent and summed in bfloat16 or wider, within the bound.
A program may use at most 128 MiB of HBM per device.

```python
import math
import jax
import jax.numpy as jnp
from jax import lax

BLOCK = 128
NT = 512
F = 128
LAGS = 128
REACH = 16
B_DEV = 4
PO = 32
NB = 256
CHANNELS = 32768
NSEG = 32
NPAIRS = 2048
N_CHAN = 64


def draw_block_pairs(key, part):
    key_first, key_second = jax.random.split(jax.random.fold_in(key, 11))
    owner = jnp.arange(NPAIRS, dtype=jnp.int32) // PO
    low = jnp.maximum(owner * B_DEV - REACH, 0)
    high = jnp.minimum(owner * B_DEV + B_DEV + REACH, NB) - 1
    first = owner * B_DEV + jax.random.randint(key_first, (NPAIRS,), -REACH, B_DEV + REACH)
    first = jnp.clip(first, low, high)
    second = first + jax.random.randint(key_second, (NPAIRS,), -REACH, REACH + 1)
    second = jnp.clip(second, low, high)
    return jnp.stack([first, second], axis=1).astype(jnp.int32)


def draw_slot_count(key, part):
    key_count, key_spot = jax.random.split(jax.random.fold_in(key, 23))
    counts = jax.random.randint(key_count, (N_CHAN,), 1, PO + 1)
    spot = jax.random.randint(key_spot, (), 0, N_CHAN)
    return jnp.where(jnp.arange(N_CHAN) == spot, PO, counts).astype(jnp.int32)


def with_ends(array, rng, low, top_value):
    longest = array.shape.index(max(array.shape))
    spots = []
    for shift in (0, 1):
        where = [jax.random.randint(jax.random.fold_in(rng, axis), (), 0, length) for axis, length in enumerate(array.shape)]
        where[longest] = (where[longest] + shift) % array.shape[longest]
        spots.append(tuple(where))
    return array.at[spots[0]].set(low).at[spots[1]].set(top_value)


def levels(own_key, dims, pieces, least, largest):
    def one(dim, parts):
        steps = jax.random.uniform(jax.random.fold_in(jax.random.fold_in(own_key, 6), dim), (parts,), jnp.float32, least / len(pieces), largest / len(pieces))
        return jnp.repeat(jnp.exp(steps), dims[dim] // parts).reshape((-1,) + (1,) * (len(dims) - dim - 1))

    factor_of = one(*pieces[0])
    for cut in pieces[1:]:
        factor_of = factor_of * one(*cut)
    return factor_of


def bell_draw(rng, dims, deviation, most, shards=(), held_as=jnp.bfloat16):
    drawn = jax.random.normal(rng, dims, jnp.float32) * deviation
    if len(shards) > 0:
        drawn = levels(rng, dims, shards, -0.22, 0.18) * drawn
    return jnp.clip(drawn, min=-most, max=most).astype(held_as)


def setup_inputs(seed: int = 0) -> dict:
    arg_keys = jax.random.split(jax.random.key(seed), 6)
    return {
        "records": bell_draw(arg_keys[0], (NSEG, CHANNELS, NT), 1.0, 6.0, ((0, 8), (1, 64))),
        "block_pairs": draw_block_pairs(jax.random.fold_in(arg_keys[5], 71), 0),
        "lag_low": with_ends(jax.random.randint(arg_keys[2], (NPAIRS,), 0, LAGS // 4), jax.random.fold_in(arg_keys[2], 1), 0, (LAGS // 4) - 1).astype(jnp.int32),
        "lag_high": with_ends(jax.random.randint(arg_keys[3], (NPAIRS,), 3 * LAGS // 4 + 1, LAGS + 1), jax.random.fold_in(arg_keys[3], 1), 3 * LAGS // 4 + 1, LAGS).astype(jnp.int32),
        "slot_count": draw_slot_count(jax.random.fold_in(arg_keys[5], 71), 0),
    }


def forward_table(length, bins):
    first = length // 32
    times = jnp.arange(length, dtype=jnp.int32)[:, None]
    freqs = (first + jnp.arange(bins, dtype=jnp.int32))[None, :]
    phase = 2.0 * math.pi / length * (times * freqs % length).astype(jnp.float32)
    return jnp.concatenate([jnp.cos(phase), -jnp.sin(phase)], axis=1).astype(jnp.bfloat16)

def inverse_table(length, bins, lag_total):
    first = length // 32
    freqs = (first + jnp.arange(bins, dtype=jnp.int32))[:, None]
    shifts = (jnp.arange(lag_total, dtype=jnp.int32) - lag_total // 2)[None, :]
    phase = 2.0 * math.pi / length * (freqs * shifts % length).astype(jnp.float32)
    return jnp.concatenate([jnp.cos(phase), -jnp.sin(phase)], axis=0)

def whiten(spectra, bins):
    real_part = spectra[..., :bins]
    imag_part = spectra[..., bins:]
    power = real_part * real_part + imag_part * imag_part
    level = lax.optimization_barrier(jnp.mean(power, axis=-1, keepdims=True))
    factor = lax.rsqrt(power + 0.1 * level + 1e-06)
    return jnp.concatenate([real_part * factor, imag_part * factor], axis=-1).astype(jnp.bfloat16)

def cross_spectrum(first, second, bins, seg_axis):
    first = first.astype(jnp.float32)
    second = second.astype(jnp.float32)
    first_re, first_im = (first[..., :bins], first[..., bins:])
    second_re, second_im = (second[..., :bins], second[..., bins:])
    real_sum = lax.optimization_barrier(jnp.sum(first_re * second_re + first_im * second_im, axis=seg_axis))
    imag_sum = lax.optimization_barrier(jnp.sum(first_re * second_im - first_im * second_re, axis=seg_axis))
    return jnp.concatenate([real_sum, imag_sum], axis=-1)

def reference(records, block_pairs, lag_low, lag_high, slot_count):
    forward = forward_table(NT, F)

    def transform(segment):
        return whiten(jnp.dot(segment, forward, preferred_element_type=jnp.float32), F)
    whitened = lax.map(transform, records)
    inverse = inverse_table(NT, F, LAGS)
    factor = 1.0 / math.sqrt(F * NSEG)
    lag_index = jnp.arange(LAGS, dtype=jnp.int32)

    def one_pair(index):
        first = lax.dynamic_slice_in_dim(whitened, (block_pairs[index, 0] * BLOCK).astype(jnp.int32), BLOCK, 1)
        second = lax.dynamic_slice_in_dim(whitened, (block_pairs[index, 1] * BLOCK).astype(jnp.int32), BLOCK, 1)
        spectrum = cross_spectrum(first, second, F, 0)
        stack = jnp.dot(spectrum, inverse, precision=lax.Precision.HIGHEST, preferred_element_type=jnp.float32) * factor
        used = index % PO < slot_count[index // PO]
        keep = (lag_index >= lag_low[index]) & (lag_index < lag_high[index]) & used
        return jnp.where(keep[None, :], stack, jnp.zeros_like(stack))
    return lax.map(one_pair, jnp.arange(NPAIRS, dtype=jnp.int32))
```

```python
import math

import jax
import jax.numpy as jnp
import ml_dtypes
import numpy as np
from jax import lax
from jax.experimental import pallas as pl
from jax.experimental.pallas import tpu as pltpu
from jax.sharding import PartitionSpec as P

BLOCK = 128
NT = 512
F = 128
LAGS = 128
B_DEV = 4
PO = 32
NX = 8
NY = 8
SEGS = 4
ROWS = 16
NBLK = 64
MESH = pl.DeviceIdType.MESH
DISTANCES = (0, 1, -1, 2, -2, 3, -3, 4)


def forward_table():
    times = np.arange(NT, dtype=np.int64)[:, None]
    freqs = (NT // 32 + np.arange(F, dtype=np.int64))[None, :]
    phase = 2.0 * math.pi / NT * (times * freqs % NT)
    table = np.concatenate([np.cos(phase), -np.sin(phase)], axis=1)
    return table.astype(np.float32).astype(ml_dtypes.bfloat16)


def inverse_table():
    freqs = (NT // 32 + np.arange(F, dtype=np.int64))[:, None]
    shifts = (np.arange(LAGS, dtype=np.int64) - LAGS // 2)[None, :]
    phase = 2.0 * math.pi / NT * (freqs * shifts % NT)
    table = np.concatenate([np.cos(phase), -np.sin(phase)], axis=0)
    return (table / math.sqrt(F * SEGS * NY)).astype(np.float32)


def spectra_kernel(x_ref, fwd_ref, out_ref, re_s, im_s):
    x = x_ref[...].reshape(SEGS * BLOCK, NT)
    spec = jnp.dot(x, fwd_ref[...], preferred_element_type=jnp.float32)
    re, im = spec[:, :F], spec[:, F:]
    power = re * re + im * im
    level = jnp.mean(power, axis=-1, keepdims=True)
    factor = lax.rsqrt(power + 0.1 * level + 1e-06)
    re, im = re * factor, im * factor
    for seg in range(SEGS):
        re_s[pl.ds(seg, BLOCK, stride=SEGS), :] = re[seg * BLOCK : (seg + 1) * BLOCK]
        im_s[pl.ds(seg, BLOCK, stride=SEGS), :] = im[seg * BLOCK : (seg + 1) * BLOCK]
    both = jnp.concatenate(
        [re_s[...].reshape(NX * NY, 8, F), im_s[...].reshape(NX * NY, 8, F)], axis=1
    )
    out_ref[...] = both.astype(jnp.bfloat16).reshape(NX * NY, 1, ROWS, F)


def spectra(records):
    fwd = jnp.asarray(forward_table())
    return pl.pallas_call(
        spectra_kernel,
        grid=(B_DEV,),
        out_shape=jax.ShapeDtypeStruct((NX * NY, B_DEV, ROWS, F), jnp.bfloat16),
        in_specs=[
            pl.BlockSpec((SEGS, BLOCK, NT), lambda b: (0, b, 0)),
            pl.BlockSpec((NT, 2 * F), lambda b: (0, 0)),
        ],
        out_specs=pl.BlockSpec((NX * NY, 1, ROWS, F), lambda b: (0, b, 0, 0)),
        scratch_shapes=[pltpu.VMEM((SEGS * BLOCK, F), jnp.float32)] * 2,
    )(records, fwd)


def remote(src, dst, send, recv, chan, win):
    return pltpu.make_async_remote_copy(
        src_ref=src,
        dst_ref=dst,
        send_sem=send,
        recv_sem=recv,
        device_id=(chan, win),
        device_id_type=MESH,
    )


def place():
    chan = lax.axis_index("chan")
    win = lax.axis_index("win")
    xc = lax.rem(chan, NX)
    return chan, win, xc, chan - xc


def greet(chan, win, xc, row, z_too):
    barrier = pltpu.get_barrier_semaphore()
    for step in range(1, NY):
        pl.semaphore_signal(
            barrier, inc=1, device_id=(chan, lax.rem(win + step, NY)), device_id_type=MESH
        )
    for step in range(1, NX):
        pl.semaphore_signal(
            barrier, inc=1, device_id=(row + lax.rem(xc + step, NX), win), device_id_type=MESH
        )
    count = NY + NX - 2
    if z_too:
        total = lax.axis_size("chan")
        for step in (NX, total - NX):
            pl.semaphore_signal(
                barrier, inc=1, device_id=(lax.rem(chan + step, total), win), device_id_type=MESH
            )
        count += 2
    pl.semaphore_wait(barrier, count)


def spread_kernel(
    s_ref, p_ref, d_ref, pg_ref, e_ref,
    y_send, y_recv, x_send, x_recv, own_sem, z_send, z_recv, p_send, p_recv, p_own,
):
    chan, win, xc, row = place()
    total = lax.axis_size("chan")
    up, down = lax.rem(chan + NX, total), lax.rem(chan + total - NX, total)
    greet(chan, win, xc, row, True)

    y_copies = []
    for k, dist in enumerate(DISTANCES):
        if k:
            to = lax.rem(win + dist + NY, NY)
            copy = remote(s_ref.at[to], e_ref.at[win], y_send.at[k], y_recv.at[win], chan, to)
            copy.start()
            y_copies.append(copy)

    pairs_own = pltpu.make_async_copy(p_ref, pg_ref.at[xc], p_own)
    pairs_own.start()
    for step in range(1, NX):
        other = row + lax.rem(xc + step, NX)
        remote(p_ref, pg_ref.at[xc], p_send.at[step], p_recv.at[step], other, win).start()

    own_first = 16 + xc * B_DEV
    owns = []
    z_copies = []

    def finish(src):
        many = d_ref.at[src, pl.ds(0, (NX - 1) * B_DEV)]
        remote(many, many, x_send.at[src], x_recv.at[src], chan, win).wait_recv()
        owns[-1].wait()

    def pass_on(src):
        for side, (lo, there, to) in enumerate(((16, 48, down), (32, 0, up))):
            copy = remote(
                d_ref.at[src, pl.ds(lo, 16)], d_ref.at[src, pl.ds(there, 16)],
                z_send.at[src, side], z_recv.at[src, side], to, win,
            )
            copy.start()
            z_copies.append(copy)

    previous = None
    for k, dist in enumerate(DISTANCES):
        src = lax.rem(win + dist + NY, NY)
        if k:
            remote(s_ref.at[src], e_ref.at[src], y_send.at[k], y_recv.at[src], chan, src).wait_recv()
        held = e_ref.at[src] if k else s_ref.at[src]
        for step in range(1, NX):
            to = lax.rem(xc + step, NX)
            remote(
                held.at[to], d_ref.at[src, pl.ds(own_first, B_DEV)],
                x_send.at[src], x_recv.at[src], row + to, win,
            ).start()
        own = pltpu.make_async_copy(
            held.at[xc], d_ref.at[src, pl.ds(own_first, B_DEV)], own_sem.at[k]
        )
        own.start()
        if previous is not None:
            finish(previous)
            pass_on(previous)
        owns.append(own)
        previous = src
    finish(previous)
    pass_on(previous)

    for copy in z_copies:
        copy.wait()
    for copy in y_copies:
        copy.wait_send()
    for dist in DISTANCES:
        src = lax.rem(win + dist + NY, NY)
        many = d_ref.at[src, pl.ds(0, (NX - 1) * B_DEV)]
        remote(many, many, x_send.at[src], x_recv.at[src], chan, win).wait_send()
    pairs_own.wait()
    for step in range(1, NX):
        frm = lax.rem(xc + NX - step, NX)
        copy = remote(p_ref, pg_ref.at[frm], p_send.at[step], p_recv.at[step], row + frm, win)
        copy.wait()


def spread(slices, pairs):
    dma = pltpu.SemaphoreType.DMA
    any_spec = pl.BlockSpec(memory_space=pl.ANY)
    return pl.pallas_call(
        spread_kernel,
        out_shape=[
            jax.ShapeDtypeStruct((NY, NBLK, ROWS, F), jnp.bfloat16),
            jax.ShapeDtypeStruct((NX, 8, 128), jnp.int32),
        ],
        in_specs=[any_spec, any_spec],
        out_specs=[any_spec, any_spec],
        scratch_shapes=[
            pltpu.VMEM((NY, NX, B_DEV, ROWS, F), jnp.bfloat16),
            dma((NY,)), dma((NY,)), dma((NY,)), dma((NY,)), dma((NY,)),
            dma((NY, 2)), dma((NY, 2)), dma((NX,)), dma((NX,)), dma(()),
        ],
        compiler_params=pltpu.CompilerParams(collective_id=0, has_side_effects=True),
    )(slices, pairs)


def pair_kernel(p_ref, d_ref, inv_ref, t_ref, re_s, im_s):
    def owner(o, carry):
        def slot(j, carry):
            a, b = p_ref[o * 8, j], p_ref[o * 8, PO + j]
            real = jnp.zeros((8, F), jnp.float32)
            imag = jnp.zeros((8, F), jnp.float32)
            for y in range(NY):
                first = d_ref[y, a].astype(jnp.float32)
                second = d_ref[y, b].astype(jnp.float32)
                a_re, a_im, b_re, b_im = first[:8], first[8:], second[:8], second[8:]
                real += a_re * b_re + a_im * b_im
                imag += a_re * b_im - a_im * b_re
            at = pl.ds(pl.multiple_of((o * PO + j) * 8, 8), 8)
            re_s[at, :] = real
            im_s[at, :] = imag
            return carry

        return lax.fori_loop(0, p_ref[o * 8, 2 * PO], slot, carry)

    lax.fori_loop(0, NX, owner, 0)
    count = NX * PO * 2
    cross = jnp.concatenate(
        [sum(s[pl.ds(seg, count, stride=SEGS), :] for seg in range(SEGS)) for s in (re_s, im_s)],
        axis=1,
    )
    stack = jnp.dot(
        cross, inv_ref[...], precision=lax.Precision.HIGHEST, preferred_element_type=jnp.float32
    ).reshape(NX, NY, 8, LAGS)
    for y in range(NY):
        t_ref[y] = stack[:, y]


def pair_stacks(gathered, blocks):
    inverse = jnp.asarray(inverse_table())
    rows = NX * PO * 8
    return pl.pallas_call(
        pair_kernel,
        out_shape=jax.ShapeDtypeStruct((NY, NX, 8, LAGS), jnp.float32),
        in_specs=[
            pl.BlockSpec(memory_space=pltpu.SMEM),
            pl.BlockSpec(memory_space=pltpu.VMEM),
            pl.BlockSpec(memory_space=pltpu.VMEM),
        ],
        out_specs=pl.BlockSpec(memory_space=pltpu.VMEM),
        scratch_shapes=[pltpu.VMEM((rows, F), jnp.float32)] * 2,
    )(gathered.reshape(NX * 8, 128), blocks, inverse)


def collect_kernel(t_ref, v_ref, u_ref, x_send, x_recv, x_own, y_send, y_recv, y_own):
    chan, win, xc, row = place()
    greet(chan, win, xc, row, False)
    own = pltpu.make_async_copy(t_ref.at[:, xc], u_ref.at[xc], x_own)
    own.start()
    copies = []
    for step in range(1, NX):
        to = lax.rem(xc + step, NX)
        copy = remote(
            t_ref.at[:, to], u_ref.at[xc], x_send.at[step], x_recv.at[step], row + to, win
        )
        copy.start()
        copies.append(copy)
    own.wait()
    for copy in copies:
        copy.wait()
    own = pltpu.make_async_copy(u_ref.at[:, win], v_ref.at[win], y_own)
    own.start()
    copies = []
    for k, dist in enumerate(DISTANCES):
        if k:
            to = lax.rem(win + dist + NY, NY)
            copy = remote(
                u_ref.at[:, to], v_ref.at[win], y_send.at[k], y_recv.at[k], chan, to
            )
            copy.start()
            copies.append(copy)
    own.wait()
    for copy in copies:
        copy.wait()


def collect(stacks):
    dma = pltpu.SemaphoreType.DMA
    any_spec = pl.BlockSpec(memory_space=pl.ANY)
    return pl.pallas_call(
        collect_kernel,
        out_shape=jax.ShapeDtypeStruct((NY, NX, 8, LAGS), jnp.float32),
        in_specs=[any_spec],
        out_specs=any_spec,
        scratch_shapes=[
            pltpu.VMEM((NX, NY, 8, LAGS), jnp.float32),
            dma((NX,)), dma((NX,)), dma(()), dma((NY,)), dma((NY,)), dma(()),
        ],
        compiler_params=pltpu.CompilerParams(collective_id=1, has_side_effects=True),
    )(stacks)


def mask_kernel(low_ref, high_ref, used_ref, v_ref, out_ref):
    lag = lax.broadcasted_iota(jnp.int32, (NX * NY, LAGS), 1)
    start = lax.axis_index("win") * B_DEV
    for slot in range(PO // NY):
        here = start + slot
        high = jnp.where(here < used_ref[0], high_ref[here], 0)
        keep = (lag >= low_ref[here]) & (lag < high)
        for c in range(2):
            rows = v_ref[pl.ds(slot * 2 + c, NX * NY, stride=8), :]
            out_ref[pl.ds(slot * BLOCK + c, NX * NY, stride=2), :] = jnp.where(keep, rows, 0.0)


def masked(lag_low, lag_high, slot_count, collected):
    smem = pl.BlockSpec(memory_space=pltpu.SMEM)
    vmem = pl.BlockSpec(memory_space=pltpu.VMEM)
    share = PO // NY
    return pl.pallas_call(
        mask_kernel,
        out_shape=jax.ShapeDtypeStruct((share * BLOCK, LAGS), jnp.float32),
        in_specs=[smem, smem, smem, vmem],
        out_specs=vmem,
    )(lag_low, lag_high, slot_count, collected.reshape(NX * NY * 8, LAGS)).reshape(
        share, BLOCK, LAGS
    )


def per_device(records, block_pairs, lag_low, lag_high, slot_count):
    chan = lax.axis_index("chan")
    base = chan // NX * NX * B_DEV - 16
    packed = jnp.concatenate([block_pairs[:, 0] - base, block_pairs[:, 1] - base, slot_count])
    pairs = jnp.pad(packed, (0, 8 * 128 - packed.shape[0])).reshape(8, 128)
    slices = spectra(records).reshape(NY, NX, B_DEV, ROWS, F)
    blocks, gathered = spread(slices, pairs)
    stacks = pair_stacks(gathered, blocks)
    return masked(lag_low, lag_high, slot_count, collect(stacks))


def solution(mesh):
    in_specs = (P("win", "chan", None), P("chan", None), P("chan"), P("chan"), P("chan"))
    out_specs = P(("chan", "win"), None, None)
    return jax.shard_map(
        per_device, mesh=mesh, in_specs=in_specs, out_specs=out_specs, check_vma=False
    )
```

```python
import math

import jax
import jax.numpy as jnp
import ml_dtypes
import numpy as np
from jax import lax
from jax.experimental import pallas as pl
from jax.experimental.pallas import tpu as pltpu
from jax.sharding import PartitionSpec as P

BLOCK = 128
NT = 512
F = 128
LAGS = 128
B_DEV = 4
PO = 32
NX = 8
NY = 8
SEGS = 4
ROWS = 16
NBLK = 64
MESH = pl.DeviceIdType.MESH
DISTANCES = (4, 3, -3, 0, 2, -2, 1, -1)
BACK = (0, 2, 1, 3, 5, 4, 7, 6)
FAR, OWN, EARLY = 3, 3, 4
OUT_ORDER = (0, 1, 2, 4, 5, 6, 7, 3)


def forward_table():
    times = np.arange(NT, dtype=np.int64)[:, None]
    freqs = (NT // 32 + np.arange(F, dtype=np.int64))[None, :]
    phase = 2.0 * math.pi / NT * (times * freqs % NT)
    table = np.concatenate([np.cos(phase), -np.sin(phase)], axis=1)
    return table.astype(np.float32).astype(ml_dtypes.bfloat16)


def inverse_table():
    freqs = (NT // 32 + np.arange(F, dtype=np.int64))[:, None]
    shifts = (np.arange(LAGS, dtype=np.int64) - LAGS // 2)[None, :]
    phase = 2.0 * math.pi / NT * (freqs * shifts % NT)
    table = np.concatenate([np.cos(phase), -np.sin(phase)], axis=0)
    return (table / math.sqrt(F * SEGS * NY)).astype(np.float32)


def remote(src, dst, send, recv, chan, win):
    return pltpu.make_async_remote_copy(
        src_ref=src,
        dst_ref=dst,
        send_sem=send,
        recv_sem=recv,
        device_id=(chan, win),
        device_id_type=MESH,
    )


def kernel(
    x_ref, fwd_ref, inv_ref, low_ref, high_ref, used_ref, pairs_ref,
    out_ref,
    x_buf, fwd_buf, inv_buf, low_s, high_s, used_s, re_s, im_s, slices, far_in, near_in,
    early, late, re_acc, im_acc, pair_buf, pair_idx, stacks, stacks_in, rows_in,
    load_sem, yf_send, yf_recv, xf_send, xf_recv, xf_own, xn_send, xn_recv, xn_own,
    yn_send, yn_recv, z_send, z_recv, p_send, p_recv, p_own,
    yo_send, yo_recv, xo_send, xo_recv, xo_own,
):
    blocks = [early.at[k] if k < EARLY else late.at[k - EARLY] for k in range(NY)]
    chan, win = lax.axis_index("chan"), lax.axis_index("win")
    total = lax.axis_size("chan")
    xc = lax.rem(chan, NX)
    row = chan - xc
    has_down, has_up = chan >= NX, chan < total - NX
    down, up = jnp.maximum(chan - NX, 0), jnp.minimum(chan + NX, total - 1)

    def y_at(k):
        return lax.rem(win + DISTANCES[k] + NY, NY)

    def x_at(step):
        return lax.rem(xc + step, NX)

    others = [k for k in range(NY) if k != OWN]
    barrier = pltpu.get_barrier_semaphore()
    for k in others:
        pl.semaphore_signal(barrier, inc=1, device_id=(chan, y_at(k)), device_id_type=MESH)
    for step in range(1, NX):
        pl.semaphore_signal(barrier, inc=1, device_id=(row + x_at(step), win), device_id_type=MESH)
    for there, to in ((has_down, down), (has_up, up)):

        @pl.when(there)
        def _():
            pl.semaphore_signal(barrier, inc=1, device_id=(to, win), device_id_type=MESH)

    loads = []
    for source, buffer in (
        (fwd_ref, fwd_buf),
        *[(x_ref.at[:, pl.ds(b * BLOCK, BLOCK)], x_buf.at[b]) for b in range(B_DEV)],
        (inv_ref, inv_buf), (low_ref, low_s), (high_ref, high_s), (used_ref, used_s),
    ):
        loads.append(pltpu.make_async_copy(source, buffer, load_sem.at[len(loads)]))
        loads[-1].start()

    local = (pairs_ref[...] - (row * B_DEV - 16)) & (NBLK - 1)
    my_pairs = pl.ds(pl.multiple_of(xc * 8, 8), 8)
    pair_buf[my_pairs, :] = jnp.concatenate(
        [
            jnp.concatenate([local, jnp.zeros((2, 128 - PO), jnp.int32)], axis=1),
            jnp.zeros((6, 128), jnp.int32),
        ],
        axis=0,
    )

    def transform(b):
        spec = jnp.dot(
            x_buf[b].reshape(SEGS * BLOCK, NT), fwd_buf[...], preferred_element_type=jnp.float32
        )
        re, im = spec[:, :F], spec[:, F:]
        power = re * re + im * im
        level = jnp.mean(power, axis=-1, keepdims=True)
        factor = lax.rsqrt(power + 0.1 * level + 1e-06)
        re, im = re * factor, im * factor
        for seg in range(SEGS):
            re_s[pl.ds(seg, BLOCK, stride=SEGS), :] = re[seg * BLOCK : (seg + 1) * BLOCK]
            im_s[pl.ds(seg, BLOCK, stride=SEGS), :] = im[seg * BLOCK : (seg + 1) * BLOCK]
        both = jnp.concatenate(
            [re_s[...].reshape(NX * NY, 8, F), im_s[...].reshape(NX * NY, 8, F)], axis=1
        )
        slices[:, :, b] = both.astype(jnp.bfloat16).reshape(NY, NX, ROWS, F)

    far_copies = []

    def send_far(b):
        for k in range(FAR):
            copy = remote(
                slices.at[y_at(k), :, b], far_in.at[BACK[k], :, b],
                yf_send.at[k, b], yf_recv.at[BACK[k], b], chan, y_at(k),
            )
            copy.start()
            far_copies.append(copy)

    own_place = pl.ds((4 + xc) * B_DEV, B_DEV)

    def each_x(send):
        def body(step, carry):
            send(x_at(step))
            return carry

        lax.fori_loop(1, NX, body, 0)

    def send_near(half):
        lo = half * 2
        for k in range(EARLY, NY):
            n = k - EARLY
            there = pl.ds(xc * B_DEV + lo, 2)

            def send(to):
                remote(
                    slices.at[y_at(k), to, pl.ds(lo, 2)], near_in.at[n, there],
                    xn_send.at[n], xn_recv.at[n], row + to, win,
                ).start()

            each_x(send)
            pltpu.make_async_copy(
                slices.at[y_at(k), xc, pl.ds(lo, 2)], near_in.at[n, there], xn_own.at[n, half]
            ).start()

    def spread_x(k):
        held = far_in.at[k] if k < FAR else slices.at[win]

        def send(to):
            remote(
                held.at[to], blocks[k].at[own_place], xf_send.at[k], xf_recv.at[k], row + to, win
            ).start()

        each_x(send)
        pltpu.make_async_copy(held.at[xc], blocks[k].at[own_place], xf_own.at[k]).start()

    loads[0].wait()
    for b in range(B_DEV):
        loads[1 + b].wait()
        transform(b)
        if b == 0:
            pl.semaphore_wait(
                barrier, NY + NX - 2 + has_down.astype(jnp.int32) + has_up.astype(jnp.int32)
            )
        send_far(b)
        if b % 2:
            send_near(b // 2)
    spread_x(OWN)
    p_copies = []
    for step in range(1, NX):
        p_copies.append(
            remote(
                pair_buf.at[my_pairs], pair_buf.at[my_pairs], p_send.at[step], p_recv.at[step],
                row + x_at(step), win,
            )
        )
        p_copies[-1].start()

    def near_all(n):
        many = near_in.at[n, pl.ds(0, (NX - 1) * B_DEV)]
        return remote(many, many, xn_send.at[n], xn_recv.at[n], chan, win)

    row_place = pl.ds(16, NX * B_DEV)
    near_copies = []
    for k in range(EARLY, NY):
        n = k - EARLY
        near_all(n).wait_recv()
        for half in range(2):
            part = pl.ds(xc * B_DEV + half * 2, 2)
            pltpu.make_async_copy(
                slices.at[y_at(k), xc, pl.ds(half * 2, 2)], near_in.at[n, part], xn_own.at[n, half]
            ).wait()
        copy = remote(
            near_in.at[n], blocks[BACK[k]].at[row_place], yn_send.at[n],
            yn_recv.at[BACK[k] - EARLY], chan, y_at(k),
        )
        copy.start()
        near_copies.append(copy)

    def halo_copy(k, side):
        lo, there, to = ((16, 48, down), (32, 0, up))[side]
        return remote(
            blocks[k].at[pl.ds(lo, 16)], blocks[k].at[pl.ds(there, 16)],
            z_send.at[k, side], z_recv.at[k, side], to, win,
        )

    def halo(k):
        for side, there in enumerate((has_down, has_up)):

            @pl.when(there)
            def _():
                halo_copy(k, side).start()

    def halo_wait(k):
        for side, there in enumerate((has_up, has_down)):

            @pl.when(there)
            def _():
                halo_copy(k, side).wait_recv()

    def spread_all(k):
        many = blocks[k].at[pl.ds(0, (NX - 1) * B_DEV)]
        return remote(many, many, xf_send.at[k], xf_recv.at[k], chan, win)

    def row_there(k):
        spread_all(k).wait_recv()
        pltpu.make_async_copy(
            slices.at[win, xc], blocks[k].at[own_place], xf_own.at[k]
        ).wait()
        halo(k)

    row_there(OWN)
    for k in (1, 2, 0):
        for b in range(B_DEV):
            remote(
                slices.at[0, :, b], far_in.at[k, :, b], yf_send.at[k, b], yf_recv.at[k, b],
                chan, y_at(k),
            ).wait_recv()
        spread_x(k)

    for step in range(1, NX):
        frm = lax.rem(xc + NX - step, NX)
        theirs = pl.ds(pl.multiple_of(frm * 8, 8), 8)
        remote(
            pair_buf.at[theirs], pair_buf.at[theirs], p_send.at[step], p_recv.at[step],
            row + frm, win,
        ).wait_recv()
    to_smem = pltpu.make_async_copy(pair_buf, pair_idx, p_own)
    to_smem.start()
    to_smem.wait()

    for k in (1, 2, 0):
        row_there(k)
    for k in range(EARLY, NY):
        remote(
            near_in.at[0], blocks[k].at[row_place], yn_send.at[k - EARLY], yn_recv.at[k - EARLY],
            chan, y_at(k),
        ).wait_recv()
        halo(k)

    def accumulate(held, y, more):
        def owner(o, carry):
            for q in range(PO // NY):
                j = y * (PO // NY) + q
                a, b = pair_idx[o * 8, j], pair_idx[o * 8 + 1, j]
                first = held[:, a].astype(jnp.float32)
                second = held[:, b].astype(jnp.float32)
                a_re, a_im, b_re, b_im = first[:, :8], first[:, 8:], second[:, :8], second[:, 8:]
                real = jnp.sum(a_re * b_re + a_im * b_im, axis=0)
                imag = jnp.sum(a_re * b_im - a_im * b_re, axis=0)
                at = pl.ds(pl.multiple_of((y * PO + o * 4 + q) * 8, 8), 8)
                if more:
                    real, imag = re_acc[at, :] + real, im_acc[at, :] + imag
                re_acc[at, :] = real
                im_acc[at, :] = imag
            return carry

        lax.fori_loop(0, NX, owner, 0)

    for k in range(EARLY):
        halo_wait(k)

    def first_half(y, carry):
        accumulate(early, y, False)
        return carry

    lax.fori_loop(0, NY, first_half, 0)
    for k in range(EARLY, NY):
        halo_wait(k)

    loads[1 + B_DEV].wait()
    out_copies = {}
    for k in OUT_ORDER:
        y = y_at(k)
        accumulate(late, y, True)
        at = y * (PO * 8)
        cross = jnp.concatenate(
            [
                sum(s[pl.ds(at + seg, NX * 8, stride=SEGS), :] for seg in range(SEGS))
                for s in (re_acc, im_acc)
            ],
            axis=1,
        )
        stacks[y] = jnp.dot(
            cross, inv_buf[...], precision=lax.Precision.HIGHEST, preferred_element_type=jnp.float32
        ).reshape(NX, 8, LAGS)
        if k != OWN:
            out_copies[k] = remote(
                stacks.at[y], stacks_in.at[BACK[k]], yo_send.at[k], yo_recv.at[BACK[k]], chan, y
            )
            out_copies[k].start()

    def rows_all(k):
        many = rows_in.at[pl.ds(0, (NX - 1) * 8)]
        return remote(many, many, xo_send.at[k], xo_recv.at[k], chan, win)

    outs = []
    for k in (OWN, 6, 7, 4, 5, 1, 2, 0):
        if k != OWN:
            remote(
                stacks.at[0], stacks_in.at[k], yo_send.at[k], yo_recv.at[k], chan, y_at(k)
            ).wait_recv()
        held = stacks.at[win] if k == OWN else stacks_in.at[k]
        place = pl.ds(pl.multiple_of((y_at(k) * NX + xc) * 8, 8), 8)

        def send(to):
            remote(
                held.at[to], rows_in.at[place], xo_send.at[k], xo_recv.at[k], row + to, win
            ).start()

        each_x(send)
        outs.append(pltpu.make_async_copy(held.at[xc], rows_in.at[place], xo_own.at[k]))
        outs[-1].start()
    for own in outs:
        own.wait()
    for k in range(NY):
        rows_all(k).wait_recv()

    for load in loads[2 + B_DEV :]:
        load.wait()
    lag = lax.broadcasted_iota(jnp.int32, (NX * NY, LAGS), 1)
    for slot in range(PO // NY):
        here = win * (PO // NY) + slot
        high = jnp.where(here < used_s[0], high_s[here], 0)
        keep = (lag >= low_s[here]) & (lag < high)
        for c in range(2):
            rows = rows_in[pl.ds(slot * 2 + c, NX * NY, stride=8), :]
            out_ref[pl.ds(slot * BLOCK + c, NX * NY, stride=2), :] = jnp.where(keep, rows, 0.0)

    for copy in far_copies + near_copies + p_copies + list(out_copies.values()):
        copy.wait_send()
    for n in range(NY - EARLY):
        near_all(n).wait_send()
    for k in range(EARLY):
        spread_all(k).wait_send()
    for k in range(NY):
        rows_all(k).wait_send()
        for side, there in enumerate((has_down, has_up)):

            @pl.when(there)
            def _():
                halo_copy(k, side).wait_send()


def per_device(records, block_pairs, lag_low, lag_high, slot_count):
    dma = pltpu.SemaphoreType.DMA
    hbm = pl.BlockSpec(memory_space=pltpu.HBM)
    vmem = pl.BlockSpec(memory_space=pltpu.VMEM)
    share = PO // NY
    near = NY - EARLY
    bf16, f32, i32 = jnp.bfloat16, jnp.float32, jnp.int32
    out = pl.pallas_call(
        kernel,
        out_shape=jax.ShapeDtypeStruct((share * BLOCK, LAGS), f32),
        in_specs=[hbm] * 6 + [vmem],
        out_specs=vmem,
        scratch_shapes=[
            pltpu.VMEM((B_DEV, SEGS, BLOCK, NT), bf16),
            pltpu.VMEM((NT, 2 * F), bf16),
            pltpu.VMEM((2 * F, LAGS), f32),
            pltpu.SMEM((PO,), i32),
            pltpu.SMEM((PO,), i32),
            pltpu.SMEM((1,), i32),
            pltpu.VMEM((SEGS * BLOCK, F), f32),
            pltpu.VMEM((SEGS * BLOCK, F), f32),
            pltpu.VMEM((NY, NX, B_DEV, ROWS, F), bf16),
            pltpu.VMEM((FAR, NX, B_DEV, ROWS, F), bf16),
            pltpu.VMEM((near, NX * B_DEV, ROWS, F), bf16),
            pltpu.VMEM((EARLY, NBLK, ROWS, F), bf16),
            pltpu.VMEM((near, NBLK, ROWS, F), bf16),
            pltpu.VMEM((NX * PO * 8, F), f32),
            pltpu.VMEM((NX * PO * 8, F), f32),
            pltpu.VMEM((NX * 8, 128), i32),
            pltpu.SMEM((NX * 8, 128), i32),
            pltpu.VMEM((NY, NX, 8, LAGS), f32),
            pltpu.VMEM((NY, NX, 8, LAGS), f32),
            pltpu.VMEM((NY * NX * 8, LAGS), f32),
            dma((B_DEV + 5,)),
            dma((FAR, B_DEV)), dma((FAR, B_DEV)),
            dma((EARLY,)), dma((EARLY,)), dma((EARLY,)),
            dma((near,)), dma((near,)), dma((near, 2)),
            dma((near,)), dma((near,)),
            dma((NY, 2)), dma((NY, 2)),
            dma((NX,)), dma((NX,)), dma(()),
            dma((NY,)), dma((NY,)), dma((NY,)), dma((NY,)), dma((NY,)),
        ],
        compiler_params=pltpu.CompilerParams(
            collective_id=0, has_side_effects=True, vmem_limit_bytes=63 << 20
        ),
    )(
        records, jnp.asarray(forward_table()), jnp.asarray(inverse_table()), lag_low, lag_high,
        slot_count, block_pairs.T,
    )
    return out.reshape(share, BLOCK, LAGS)


def solution(mesh):
    in_specs = (P("win", "chan", None), P("chan", None), P("chan"), P("chan"), P("chan"))
    out_specs = P(("chan", "win"), None, None)
    return jax.shard_map(
        per_device, mesh=mesh, in_specs=in_specs, out_specs=out_specs, check_vma=False
    )
```

```python
import math

import jax
import jax.numpy as jnp
import ml_dtypes
import numpy as np
from jax import lax
from jax.experimental import pallas as pl
from jax.experimental.pallas import tpu as pltpu
from jax.sharding import PartitionSpec as P

BLOCK = 128
NT = 512
F = 128
LAGS = 128
B_DEV = 4
PO = 32
NX = 8
NY = 8
SEGS = 4
ROWS = 16
NBLK = 64
MESH = pl.DeviceIdType.MESH
DISTANCES = (4, 3, -3, 0, 2, -2, 1, -1)
BACK = (0, 2, 1, 3, 5, 4, 7, 6)
OWN, EARLY = 3, 4
OUT_ORDER = (0, 1, 2, 4, 5, 6, 7, 3)


def forward_table():
    times = np.arange(NT, dtype=np.int64)[:, None]
    freqs = (NT // 32 + np.arange(F, dtype=np.int64))[None, :]
    phase = 2.0 * math.pi / NT * (times * freqs % NT)
    table = np.concatenate([np.cos(phase), -np.sin(phase)], axis=1)
    return table.astype(np.float32).astype(ml_dtypes.bfloat16)


def inverse_table():
    freqs = (NT // 32 + np.arange(F, dtype=np.int64))[:, None]
    shifts = (np.arange(LAGS, dtype=np.int64) - LAGS // 2)[None, :]
    phase = 2.0 * math.pi / NT * (freqs * shifts % NT)
    table = np.concatenate([np.cos(phase), -np.sin(phase)], axis=0)
    return (table / math.sqrt(F * SEGS * NY)).astype(np.float32)


def remote(src, dst, send, recv, chan, win):
    return pltpu.make_async_remote_copy(
        src_ref=src,
        dst_ref=dst,
        send_sem=send,
        recv_sem=recv,
        device_id=(chan, win),
        device_id_type=MESH,
    )


def kernel(
    x_ref, fwd_ref, inv_ref, pairs_ref,
    rows_in,
    x_buf, fwd_buf, inv_buf, re_s, im_s, slices, early, late, re_acc, im_acc,
    pair_buf, pair_idx, stacks,
    load_sem, in_send, in_recv, in_own, z_send, z_recv, p_send, p_recv, p_own,
    out_send, out_recv, out_own,
):
    blocks = [early.at[k] if k < EARLY else late.at[k - EARLY] for k in range(NY)]
    chan, win = lax.axis_index("chan"), lax.axis_index("win")
    total = lax.axis_size("chan")
    xc = lax.rem(chan, NX)
    row = chan - xc
    has_down, has_up = chan >= NX, chan < total - NX
    down, up = jnp.maximum(chan - NX, 0), jnp.minimum(chan + NX, total - 1)

    def y_at(k):
        return lax.rem(win + DISTANCES[k] + NY, NY)

    def x_at(step):
        return lax.rem(xc + step, NX)

    me = win * NX + xc
    barrier = pltpu.get_barrier_semaphore()

    def call(step, carry):
        other = lax.rem(me + step, NX * NY)
        pl.semaphore_signal(
            barrier, inc=1, device_id=(row + lax.rem(other, NX), other // NX), device_id_type=MESH
        )
        return carry

    lax.fori_loop(1, NX * NY, call, 0)
    for there, to in ((has_down, down), (has_up, up)):

        @pl.when(there)
        def _():
            pl.semaphore_signal(barrier, inc=1, device_id=(to, win), device_id_type=MESH)

    loads = []
    for source, buffer in (
        (fwd_ref, fwd_buf),
        *[(x_ref.at[:, pl.ds(b * BLOCK, BLOCK)], x_buf.at[b]) for b in range(B_DEV)],
        (inv_ref, inv_buf),
    ):
        loads.append(pltpu.make_async_copy(source, buffer, load_sem.at[len(loads)]))
        loads[-1].start()

    local = (pairs_ref[...] - (row * B_DEV - 16)) & (NBLK - 1)
    my_pairs = pl.ds(pl.multiple_of(xc * 8, 8), 8)
    pair_buf[my_pairs, :] = jnp.concatenate(
        [
            jnp.concatenate([local, jnp.zeros((2, 128 - PO), jnp.int32)], axis=1),
            jnp.zeros((6, 128), jnp.int32),
        ],
        axis=0,
    )

    def transform(b):
        spec = jnp.dot(
            x_buf[b].reshape(SEGS * BLOCK, NT), fwd_buf[...], preferred_element_type=jnp.float32
        )
        re, im = spec[:, :F], spec[:, F:]
        power = re * re + im * im
        level = jnp.mean(power, axis=-1, keepdims=True)
        factor = lax.rsqrt(power + 0.1 * level + 1e-06)
        re, im = re * factor, im * factor
        for seg in range(SEGS):
            re_s[pl.ds(seg, BLOCK, stride=SEGS), :] = re[seg * BLOCK : (seg + 1) * BLOCK]
            im_s[pl.ds(seg, BLOCK, stride=SEGS), :] = im[seg * BLOCK : (seg + 1) * BLOCK]
        both = jnp.concatenate(
            [re_s[...].reshape(NX * NY, 8, F), im_s[...].reshape(NX * NY, 8, F)], axis=1
        )
        slices[:, :, b] = both.astype(jnp.bfloat16).reshape(NY, NX, ROWS, F)

    own_place = pl.ds((4 + xc) * B_DEV, B_DEV)

    def each_x(first, send):
        def body(step, carry):
            send(x_at(step))
            return carry

        lax.fori_loop(first, NX, body, 0)

    def spread(k):
        def send(to):
            remote(
                slices.at[y_at(k), to], blocks[BACK[k]].at[own_place], in_send.at[k],
                in_recv.at[BACK[k]], row + to, y_at(k),
            ).start()

        each_x(1 if k == OWN else 0, send)

    def spread_all(k):
        many = blocks[k].at[pl.ds(0, (NX - 1 if k == OWN else NX) * B_DEV)]
        return remote(many, many, in_send.at[k], in_recv.at[k], chan, y_at(k))

    loads[0].wait()
    for b in range(B_DEV):
        loads[1 + b].wait()
        transform(b)
    pl.semaphore_wait(
        barrier, NX * NY - 1 + has_down.astype(jnp.int32) + has_up.astype(jnp.int32)
    )
    for k in (0, 1, 2, OWN):
        spread(k)
    own = pltpu.make_async_copy(slices.at[win, xc], blocks[OWN].at[own_place], in_own)
    own.start()
    p_copies = []
    for step in range(1, NX):
        p_copies.append(
            remote(
                pair_buf.at[my_pairs], pair_buf.at[my_pairs], p_send.at[step], p_recv.at[step],
                row + x_at(step), win,
            )
        )
        p_copies[-1].start()

    def halo_copy(k, side):
        lo, there, to = ((16, 48, down), (32, 0, up))[side]
        return remote(
            blocks[k].at[pl.ds(lo, 16)], blocks[k].at[pl.ds(there, 16)],
            z_send.at[k, side], z_recv.at[k, side], to, win,
        )

    def halo(k):
        for side, there in enumerate((has_down, has_up)):

            @pl.when(there)
            def _():
                halo_copy(k, side).start()

    def halo_wait(k):
        for side, there in enumerate((has_up, has_down)):

            @pl.when(there)
            def _():
                halo_copy(k, side).wait_recv()

    def row_there(k):
        spread_all(k).wait_recv()
        halo(k)

    own.wait()
    row_there(OWN)
    row_there(0)
    spread(4)
    spread(5)
    row_there(1)
    row_there(2)
    spread(6)
    spread(7)

    for step in range(1, NX):
        frm = lax.rem(xc + NX - step, NX)
        theirs = pl.ds(pl.multiple_of(frm * 8, 8), 8)
        remote(
            pair_buf.at[theirs], pair_buf.at[theirs], p_send.at[step], p_recv.at[step],
            row + frm, win,
        ).wait_recv()
    to_smem = pltpu.make_async_copy(pair_buf, pair_idx, p_own)
    to_smem.start()
    to_smem.wait()

    for k in range(EARLY, NY):
        row_there(k)

    def accumulate(held, y, more):
        def owner(o, carry):
            for q in range(PO // NY):
                j = y * (PO // NY) + q
                a, b = pair_idx[o * 8, j], pair_idx[o * 8 + 1, j]
                first = held[:, a].astype(jnp.float32)
                second = held[:, b].astype(jnp.float32)
                a_re, a_im, b_re, b_im = first[:, :8], first[:, 8:], second[:, :8], second[:, 8:]
                real = jnp.sum(a_re * b_re + a_im * b_im, axis=0)
                imag = jnp.sum(a_re * b_im - a_im * b_re, axis=0)
                at = pl.ds(pl.multiple_of((y * PO + o * 4 + q) * 8, 8), 8)
                if more:
                    real, imag = re_acc[at, :] + real, im_acc[at, :] + imag
                re_acc[at, :] = real
                im_acc[at, :] = imag
            return carry

        lax.fori_loop(0, NX, owner, 0)

    for k in range(EARLY):
        halo_wait(k)

    def first_half(y, carry):
        accumulate(early, y, False)
        return carry

    lax.fori_loop(0, NY, first_half, 0)
    for k in range(EARLY, NY):
        halo_wait(k)

    loads[1 + B_DEV].wait()
    my_rows = pl.ds(pl.multiple_of(me * 8, 8), 8)
    for k in OUT_ORDER:
        y = y_at(k)
        accumulate(late, y, True)
        at = y * (PO * 8)
        cross = jnp.concatenate(
            [
                sum(s[pl.ds(at + seg, NX * 8, stride=SEGS), :] for seg in range(SEGS))
                for s in (re_acc, im_acc)
            ],
            axis=1,
        )
        stacks[y] = jnp.dot(
            cross, inv_buf[...], precision=lax.Precision.HIGHEST, preferred_element_type=jnp.float32
        ).reshape(NX, 8, LAGS)

        def send(to):
            remote(
                stacks.at[y, to], rows_in.at[my_rows], out_send.at[k], out_recv, row + to, y
            ).start()

        each_x(1 if k == OWN else 0, send)
    out_copy = pltpu.make_async_copy(stacks.at[win, xc], rows_in.at[my_rows], out_own)
    out_copy.start()

    for copy in p_copies:
        copy.wait_send()
    for k in range(NY):
        spread_all(k).wait_send()
        many = rows_in.at[pl.ds(0, (NX - 1 if k == OWN else NX) * 8)]
        remote(many, many, out_send.at[k], out_recv, chan, win).wait_send()
        for side, there in enumerate((has_down, has_up)):

            @pl.when(there)
            def _():
                halo_copy(k, side).wait_send()

    out_copy.wait()
    many = rows_in.at[pl.ds(0, (NX * NY - 1) * 8)]
    remote(many, many, out_send.at[0], out_recv, chan, win).wait_recv()


def mask_kernel(low_ref, high_ref, used_ref, v_ref, out_ref):
    lag = lax.broadcasted_iota(jnp.int32, (NX * NY, LAGS), 1)
    start = lax.axis_index("win") * (PO // NY)
    for slot in range(PO // NY):
        here = start + slot
        high = jnp.where(here < used_ref[0], high_ref[here], 0)
        keep = (lag >= low_ref[here]) & (lag < high)
        for c in range(2):
            part = v_ref[pl.ds(slot * 2 + c, NX * NY, stride=8), :]
            out_ref[pl.ds(slot * BLOCK + c, NX * NY, stride=2), :] = jnp.where(keep, part, 0.0)


def masked(lag_low, lag_high, slot_count, rows):
    smem = pl.BlockSpec(memory_space=pltpu.SMEM)
    vmem = pl.BlockSpec(memory_space=pltpu.VMEM)
    share = PO // NY
    return pl.pallas_call(
        mask_kernel,
        out_shape=jax.ShapeDtypeStruct((share * BLOCK, LAGS), jnp.float32),
        in_specs=[smem, smem, smem, vmem],
        out_specs=vmem,
    )(lag_low, lag_high, slot_count, rows).reshape(
        share, BLOCK, LAGS
    )


def per_device(records, block_pairs, lag_low, lag_high, slot_count):
    dma = pltpu.SemaphoreType.DMA
    hbm = pl.BlockSpec(memory_space=pltpu.HBM)
    vmem = pl.BlockSpec(memory_space=pltpu.VMEM)
    near = NY - EARLY
    bf16, f32, i32 = jnp.bfloat16, jnp.float32, jnp.int32
    rows = pl.pallas_call(
        kernel,
        out_shape=jax.ShapeDtypeStruct((NY * NX * 8, LAGS), f32),
        in_specs=[hbm] * 3 + [vmem],
        out_specs=hbm,
        scratch_shapes=[
            pltpu.VMEM((B_DEV, SEGS, BLOCK, NT), bf16),
            pltpu.VMEM((NT, 2 * F), bf16),
            pltpu.VMEM((2 * F, LAGS), f32),
            pltpu.VMEM((SEGS * BLOCK, F), f32),
            pltpu.VMEM((SEGS * BLOCK, F), f32),
            pltpu.VMEM((NY, NX, B_DEV, ROWS, F), bf16),
            pltpu.VMEM((EARLY, NBLK, ROWS, F), bf16),
            pltpu.VMEM((near, NBLK, ROWS, F), bf16),
            pltpu.VMEM((NX * PO * 8, F), f32),
            pltpu.VMEM((NX * PO * 8, F), f32),
            pltpu.VMEM((NX * 8, 128), i32),
            pltpu.SMEM((NX * 8, 128), i32),
            pltpu.VMEM((NY, NX, 8, LAGS), f32),
            dma((B_DEV + 2,)),
            dma((NY,)), dma((NY,)), dma(()),
            dma((NY, 2)), dma((NY, 2)),
            dma((NX,)), dma((NX,)), dma(()),
            dma((NY,)), dma(()), dma(()),
        ],
        compiler_params=pltpu.CompilerParams(
            collective_id=0, has_side_effects=True, vmem_limit_bytes=63 << 20
        ),
    )(
        records, jnp.asarray(forward_table()), jnp.asarray(inverse_table()), block_pairs.T
    )
    return masked(lag_low, lag_high, slot_count, rows)


def solution(mesh):
    in_specs = (P("win", "chan", None), P("chan", None), P("chan"), P("chan"), P("chan"))
    out_specs = P(("chan", "win"), None, None)
    return jax.shard_map(
        per_device, mesh=mesh, in_specs=in_specs, out_specs=out_specs, check_vma=False
    )
```

```python
import math

import jax
import jax.numpy as jnp
import ml_dtypes
import numpy as np
from jax import lax
from jax.experimental import pallas as pl
from jax.experimental.pallas import tpu as pltpu
from jax.sharding import PartitionSpec as P

BLOCK = 128
NT = 512
F = 128
LAGS = 128
B_DEV = 4
PO = 32
NX = 8
NY = 8
SEGS = 4
ROWS = 16
NBLK = 64
MESH = pl.DeviceIdType.MESH
DISTANCES = (1, -1, 2, 0, -2, 3, -3, 4)
BACK = (1, 0, 4, 3, 2, 6, 5, 7)
OWN, EARLY = 3, 4
OUT_ORDER = (7, 5, 6, 2, 4, 0, 1, 3)


def forward_table():
    times = np.arange(NT, dtype=np.int64)[:, None]
    freqs = (NT // 32 + np.arange(F, dtype=np.int64))[None, :]
    phase = 2.0 * math.pi / NT * (times * freqs % NT)
    table = np.concatenate([np.cos(phase), -np.sin(phase)], axis=1)
    return table.astype(np.float32).astype(ml_dtypes.bfloat16)


def inverse_table():
    freqs = (NT // 32 + np.arange(F, dtype=np.int64))[:, None]
    shifts = (np.arange(LAGS, dtype=np.int64) - LAGS // 2)[None, :]
    phase = 2.0 * math.pi / NT * (freqs * shifts % NT)
    table = np.concatenate([np.cos(phase), -np.sin(phase)], axis=0)
    return (table / math.sqrt(F * SEGS * NY)).astype(np.float32)


def remote(src, dst, send, recv, chan, win):
    return pltpu.make_async_remote_copy(
        src_ref=src,
        dst_ref=dst,
        send_sem=send,
        recv_sem=recv,
        device_id=(chan, win),
        device_id_type=MESH,
    )


def kernel(
    x_ref, fwd_ref, inv_ref, pairs_ref,
    rows_in,
    x_buf, fwd_buf, inv_buf, re_s, im_s, slices, early, late, re_acc, im_acc,
    pair_buf, pair_idx, stacks,
    load_sem, in_send, in_recv, in_own, z_send, z_recv, p_send, p_recv, p_own,
    out_send, out_recv, out_own,
):
    blocks = [early.at[k] if k < EARLY else late.at[k - EARLY] for k in range(NY)]
    chan, win = lax.axis_index("chan"), lax.axis_index("win")
    total = lax.axis_size("chan")
    xc = lax.rem(chan, NX)
    row = chan - xc
    has_down, has_up = chan >= NX, chan < total - NX
    down, up = jnp.maximum(chan - NX, 0), jnp.minimum(chan + NX, total - 1)

    def y_at(k):
        return lax.rem(win + DISTANCES[k] + NY, NY)

    def x_at(step):
        return lax.rem(xc + step, NX)

    me = win * NX + xc
    barrier = pltpu.get_barrier_semaphore()

    def call(step, carry):
        other = lax.rem(me + step, NX * NY)
        pl.semaphore_signal(
            barrier, inc=1, device_id=(row + lax.rem(other, NX), other // NX), device_id_type=MESH
        )
        return carry

    lax.fori_loop(1, NX * NY, call, 0)
    for there, to in ((has_down, down), (has_up, up)):

        @pl.when(there)
        def _():
            pl.semaphore_signal(barrier, inc=1, device_id=(to, win), device_id_type=MESH)

    loads = []
    for source, buffer in (
        (fwd_ref, fwd_buf),
        *[(x_ref.at[:, pl.ds(b * BLOCK, BLOCK)], x_buf.at[b]) for b in range(B_DEV)],
        (inv_ref, inv_buf),
    ):
        loads.append(pltpu.make_async_copy(source, buffer, load_sem.at[len(loads)]))
        loads[-1].start()

    local = (pairs_ref[...] - (row * B_DEV - 16)) & (NBLK - 1)
    my_pairs = pl.ds(pl.multiple_of(xc * 8, 8), 8)
    pair_buf[my_pairs, :] = jnp.concatenate(
        [
            jnp.concatenate([local, jnp.zeros((2, 128 - PO), jnp.int32)], axis=1),
            jnp.zeros((6, 128), jnp.int32),
        ],
        axis=0,
    )

    def transform(b):
        spec = jnp.dot(
            x_buf[b].reshape(SEGS * BLOCK, NT), fwd_buf[...], preferred_element_type=jnp.float32
        )
        re, im = spec[:, :F], spec[:, F:]
        power = re * re + im * im
        level = jnp.mean(power, axis=-1, keepdims=True)
        factor = lax.rsqrt(power + 0.1 * level + 1e-06)
        re, im = re * factor, im * factor
        for seg in range(SEGS):
            re_s[pl.ds(seg, BLOCK, stride=SEGS), :] = re[seg * BLOCK : (seg + 1) * BLOCK]
            im_s[pl.ds(seg, BLOCK, stride=SEGS), :] = im[seg * BLOCK : (seg + 1) * BLOCK]
        both = jnp.concatenate(
            [re_s[...].reshape(NX * NY, 8, F), im_s[...].reshape(NX * NY, 8, F)], axis=1
        )
        slices[:, :, b] = both.astype(jnp.bfloat16).reshape(NY, NX, ROWS, F)

    own_place = pl.ds((4 + xc) * B_DEV, B_DEV)

    def each_x(first, send):
        def body(step, carry):
            send(x_at(step))
            return carry

        lax.fori_loop(first, NX, body, 0)

    def spread(k):
        def send(to):
            remote(
                slices.at[y_at(k), to], blocks[BACK[k]].at[own_place], in_send.at[k],
                in_recv.at[BACK[k]], row + to, y_at(k),
            ).start()

        each_x(1 if k == OWN else 0, send)

    def spread_all(k):
        many = blocks[k].at[pl.ds(0, (NX - 1 if k == OWN else NX) * B_DEV)]
        return remote(many, many, in_send.at[k], in_recv.at[k], chan, y_at(k))

    loads[0].wait()
    for b in range(B_DEV):
        loads[1 + b].wait()
        transform(b)
    pl.semaphore_wait(
        barrier, NX * NY - 1 + has_down.astype(jnp.int32) + has_up.astype(jnp.int32)
    )
    for k in (0, 1, OWN, 2, 4, 5, 6, 7):
        spread(k)
    own = pltpu.make_async_copy(slices.at[win, xc], blocks[OWN].at[own_place], in_own)
    own.start()
    p_copies = []
    for step in range(1, NX):
        p_copies.append(
            remote(
                pair_buf.at[my_pairs], pair_buf.at[my_pairs], p_send.at[step], p_recv.at[step],
                row + x_at(step), win,
            )
        )
        p_copies[-1].start()

    def halo_copy(k, side):
        lo, there, to = ((16, 48, down), (32, 0, up))[side]
        return remote(
            blocks[k].at[pl.ds(lo, 16)], blocks[k].at[pl.ds(there, 16)],
            z_send.at[k, side], z_recv.at[k, side], to, win,
        )

    def halo(k):
        for side, there in enumerate((has_down, has_up)):

            @pl.when(there)
            def _():
                halo_copy(k, side).start()

    def halo_wait(k):
        for side, there in enumerate((has_up, has_down)):

            @pl.when(there)
            def _():
                halo_copy(k, side).wait_recv()

    def row_there(k):
        spread_all(k).wait_recv()
        halo(k)

    own.wait()
    for k in (0, 1, OWN, 2):
        row_there(k)

    for step in range(1, NX):
        frm = lax.rem(xc + NX - step, NX)
        theirs = pl.ds(pl.multiple_of(frm * 8, 8), 8)
        remote(
            pair_buf.at[theirs], pair_buf.at[theirs], p_send.at[step], p_recv.at[step],
            row + frm, win,
        ).wait_recv()
    to_smem = pltpu.make_async_copy(pair_buf, pair_idx, p_own)
    to_smem.start()
    to_smem.wait()

    for k in range(EARLY, NY):
        row_there(k)

    def accumulate(held, y, more):
        def owner(o, carry):
            for q in range(PO // NY):
                j = y * (PO // NY) + q
                a, b = pair_idx[o * 8, j], pair_idx[o * 8 + 1, j]
                first = held[:, a].astype(jnp.float32)
                second = held[:, b].astype(jnp.float32)
                a_re, a_im, b_re, b_im = first[:, :8], first[:, 8:], second[:, :8], second[:, 8:]
                real = jnp.sum(a_re * b_re + a_im * b_im, axis=0)
                imag = jnp.sum(a_re * b_im - a_im * b_re, axis=0)
                at = pl.ds(pl.multiple_of((y * PO + o * 4 + q) * 8, 8), 8)
                if more:
                    real, imag = re_acc[at, :] + real, im_acc[at, :] + imag
                re_acc[at, :] = real
                im_acc[at, :] = imag
            return carry

        lax.fori_loop(0, NX, owner, 0)

    for k in range(EARLY):
        halo_wait(k)

    def first_half(y, carry):
        accumulate(early, y, False)
        return carry

    lax.fori_loop(0, NY, first_half, 0)
    for k in range(EARLY, NY):
        halo_wait(k)

    loads[1 + B_DEV].wait()
    my_rows = pl.ds(pl.multiple_of(me * 8, 8), 8)
    for k in OUT_ORDER:
        y = y_at(k)
        accumulate(late, y, True)
        at = y * (PO * 8)
        cross = jnp.concatenate(
            [
                sum(s[pl.ds(at + seg, NX * 8, stride=SEGS), :] for seg in range(SEGS))
                for s in (re_acc, im_acc)
            ],
            axis=1,
        )
        stacks[y] = jnp.dot(
            cross, inv_buf[...], precision=lax.Precision.HIGHEST, preferred_element_type=jnp.float32
        ).reshape(NX, 8, LAGS)

        def send(to):
            remote(
                stacks.at[y, to], rows_in.at[my_rows], out_send.at[k], out_recv, row + to, y
            ).start()

        each_x(1 if k == OWN else 0, send)
    out_copy = pltpu.make_async_copy(stacks.at[win, xc], rows_in.at[my_rows], out_own)
    out_copy.start()

    for copy in p_copies:
        copy.wait_send()
    for k in range(NY):
        spread_all(k).wait_send()
        many = rows_in.at[pl.ds(0, (NX - 1 if k == OWN else NX) * 8)]
        remote(many, many, out_send.at[k], out_recv, chan, win).wait_send()
        for side, there in enumerate((has_down, has_up)):

            @pl.when(there)
            def _():
                halo_copy(k, side).wait_send()

    out_copy.wait()
    many = rows_in.at[pl.ds(0, (NX * NY - 1) * 8)]
    remote(many, many, out_send.at[0], out_recv, chan, win).wait_recv()


def mask_kernel(low_ref, high_ref, used_ref, v_ref, out_ref):
    lag = lax.broadcasted_iota(jnp.int32, (NX * NY, LAGS), 1)
    start = lax.axis_index("win") * (PO // NY)
    for slot in range(PO // NY):
        here = start + slot
        high = jnp.where(here < used_ref[0], high_ref[here], 0)
        keep = (lag >= low_ref[here]) & (lag < high)
        for c in range(2):
            part = v_ref[pl.ds(slot * 2 + c, NX * NY, stride=8), :]
            out_ref[pl.ds(slot * BLOCK + c, NX * NY, stride=2), :] = jnp.where(keep, part, 0.0)


def masked(lag_low, lag_high, slot_count, rows):
    smem = pl.BlockSpec(memory_space=pltpu.SMEM)
    vmem = pl.BlockSpec(memory_space=pltpu.VMEM)
    share = PO // NY
    return pl.pallas_call(
        mask_kernel,
        out_shape=jax.ShapeDtypeStruct((share * BLOCK, LAGS), jnp.float32),
        in_specs=[smem, smem, smem, vmem],
        out_specs=vmem,
    )(lag_low, lag_high, slot_count, rows).reshape(
        share, BLOCK, LAGS
    )


def per_device(records, block_pairs, lag_low, lag_high, slot_count):
    dma = pltpu.SemaphoreType.DMA
    hbm = pl.BlockSpec(memory_space=pltpu.HBM)
    vmem = pl.BlockSpec(memory_space=pltpu.VMEM)
    near = NY - EARLY
    bf16, f32, i32 = jnp.bfloat16, jnp.float32, jnp.int32
    rows = pl.pallas_call(
        kernel,
        out_shape=jax.ShapeDtypeStruct((NY * NX * 8, LAGS), f32),
        in_specs=[hbm] * 3 + [vmem],
        out_specs=hbm,
        scratch_shapes=[
            pltpu.VMEM((B_DEV, SEGS, BLOCK, NT), bf16),
            pltpu.VMEM((NT, 2 * F), bf16),
            pltpu.VMEM((2 * F, LAGS), f32),
            pltpu.VMEM((SEGS * BLOCK, F), f32),
            pltpu.VMEM((SEGS * BLOCK, F), f32),
            pltpu.VMEM((NY, NX, B_DEV, ROWS, F), bf16),
            pltpu.VMEM((EARLY, NBLK, ROWS, F), bf16),
            pltpu.VMEM((near, NBLK, ROWS, F), bf16),
            pltpu.VMEM((NX * PO * 8, F), f32),
            pltpu.VMEM((NX * PO * 8, F), f32),
            pltpu.VMEM((NX * 8, 128), i32),
            pltpu.SMEM((NX * 8, 128), i32),
            pltpu.VMEM((NY, NX, 8, LAGS), f32),
            dma((B_DEV + 2,)),
            dma((NY,)), dma((NY,)), dma(()),
            dma((NY, 2)), dma((NY, 2)),
            dma((NX,)), dma((NX,)), dma(()),
            dma((NY,)), dma(()), dma(()),
        ],
        compiler_params=pltpu.CompilerParams(
            collective_id=0, has_side_effects=True, vmem_limit_bytes=63 << 20
        ),
    )(
        records, jnp.asarray(forward_table()), jnp.asarray(inverse_table()), block_pairs.T
    )
    return masked(lag_low, lag_high, slot_count, rows)


def solution(mesh):
    in_specs = (P("win", "chan", None), P("chan", None), P("chan"), P("chan"), P("chan"))
    out_specs = P(("chan", "win"), None, None)
    return jax.shard_map(
        per_device, mesh=mesh, in_specs=in_specs, out_specs=out_specs, check_vma=False
    )
```

```python
import math

import jax
import jax.numpy as jnp
import ml_dtypes
import numpy as np
from jax import lax
from jax.experimental import pallas as pl
from jax.experimental.pallas import tpu as pltpu
from jax.sharding import PartitionSpec as P

BLOCK = 128
NT = 512
F = 128
LAGS = 128
B_DEV = 4
PO = 32
NX = 8
NY = 8
SEGS = 4
ROWS = 16
NBLK = 64
MESH = pl.DeviceIdType.MESH
DISTANCES = (1, -1, 2, 0, -2, 3, -3, 4)
BACK = (1, 0, 4, 3, 2, 6, 5, 7)
OWN, EARLY = 3, 4
OUT_ORDER = (7, 5, 6, 2, 4, 0, 1, 3)


def forward_table():
    times = np.arange(NT, dtype=np.int64)[:, None]
    freqs = (NT // 32 + np.arange(F, dtype=np.int64))[None, :]
    phase = 2.0 * math.pi / NT * (times * freqs % NT)
    table = np.concatenate([np.cos(phase), -np.sin(phase)], axis=1)
    return table.astype(np.float32).astype(ml_dtypes.bfloat16)


def inverse_table():
    freqs = (NT // 32 + np.arange(F, dtype=np.int64))[:, None]
    shifts = (np.arange(LAGS, dtype=np.int64) - LAGS // 2)[None, :]
    phase = 2.0 * math.pi / NT * (freqs * shifts % NT)
    table = np.concatenate([np.cos(phase), -np.sin(phase)], axis=0)
    return (table / math.sqrt(F * SEGS * NY)).astype(np.float32)


def remote(src, dst, send, recv, chan, win):
    return pltpu.make_async_remote_copy(
        src_ref=src,
        dst_ref=dst,
        send_sem=send,
        recv_sem=recv,
        device_id=(chan, win),
        device_id_type=MESH,
    )


def kernel(
    x_ref, fwd_ref, inv_ref, pairs_ref,
    rows_in,
    x_buf, fwd_buf, inv_buf, re_s, im_s, slices, early, late, re_acc, im_acc,
    pair_buf, pair_idx, stacks,
    load_sem, in_send, in_recv, in_own, z_send, z_recv, p_send, p_recv, p_own,
    out_send, out_recv, out_own,
):
    blocks = [early.at[k] if k < EARLY else late.at[k - EARLY] for k in range(NY)]
    chan, win = lax.axis_index("chan"), lax.axis_index("win")
    total = lax.axis_size("chan")
    xc = lax.rem(chan, NX)
    row = chan - xc
    has_down, has_up = chan >= NX, chan < total - NX
    down, up = jnp.maximum(chan - NX, 0), jnp.minimum(chan + NX, total - 1)

    def y_at(k):
        return lax.rem(win + DISTANCES[k] + NY, NY)

    def x_at(step):
        return lax.rem(xc + step, NX)

    me = win * NX + xc
    barrier = pltpu.get_barrier_semaphore()

    def call(step, carry):
        other = lax.rem(me + step, NX * NY)
        pl.semaphore_signal(
            barrier, inc=1, device_id=(row + lax.rem(other, NX), other // NX), device_id_type=MESH
        )
        return carry

    lax.fori_loop(1, NX * NY, call, 0)
    for there, to in ((has_down, down), (has_up, up)):

        @pl.when(there)
        def _():
            pl.semaphore_signal(barrier, inc=1, device_id=(to, win), device_id_type=MESH)

    loads = []
    for source, buffer in (
        (fwd_ref, fwd_buf),
        *[(x_ref.at[:, pl.ds(b * BLOCK, BLOCK)], x_buf.at[b]) for b in range(B_DEV)],
        (inv_ref, inv_buf),
    ):
        loads.append(pltpu.make_async_copy(source, buffer, load_sem.at[len(loads)]))
        loads[-1].start()

    local = (pairs_ref[...] - (row * B_DEV - 16)) & (NBLK - 1)
    my_pairs = pl.ds(pl.multiple_of(xc * 8, 8), 8)
    pair_buf[my_pairs, :] = jnp.concatenate(
        [
            jnp.concatenate([local, jnp.zeros((2, 128 - PO), jnp.int32)], axis=1),
            jnp.zeros((6, 128), jnp.int32),
        ],
        axis=0,
    )

    def transform(b):
        spec = jnp.dot(
            x_buf[b].reshape(SEGS * BLOCK, NT), fwd_buf[...], preferred_element_type=jnp.float32
        )
        re, im = spec[:, :F], spec[:, F:]
        power = re * re + im * im
        level = jnp.mean(power, axis=-1, keepdims=True)
        factor = lax.rsqrt(power + 0.1 * level + 1e-06)
        re, im = re * factor, im * factor
        for seg in range(SEGS):
            re_s[pl.ds(seg, BLOCK, stride=SEGS), :] = re[seg * BLOCK : (seg + 1) * BLOCK]
            im_s[pl.ds(seg, BLOCK, stride=SEGS), :] = im[seg * BLOCK : (seg + 1) * BLOCK]
        both = jnp.concatenate(
            [re_s[...].reshape(NX * NY, 8, F), im_s[...].reshape(NX * NY, 8, F)], axis=1
        )
        slices[:, :, b] = both.astype(jnp.bfloat16).reshape(NY, NX, ROWS, F)

    own_place = pl.ds((4 + xc) * B_DEV, B_DEV)

    def each_x(first, send):
        def body(step, carry):
            send(x_at(step))
            return carry

        lax.fori_loop(first, NX, body, 0)

    def spread(k):
        def send(to):
            remote(
                slices.at[y_at(k), to], blocks[BACK[k]].at[own_place], in_send.at[k],
                in_recv.at[BACK[k]], row + to, y_at(k),
            ).start()

        each_x(1 if k == OWN else 0, send)

    def spread_all(k):
        many = blocks[k].at[pl.ds(0, (NX - 1 if k == OWN else NX) * B_DEV)]
        return remote(many, many, in_send.at[k], in_recv.at[k], chan, y_at(k))

    loads[0].wait()
    for b in range(B_DEV):
        loads[1 + b].wait()
        transform(b)
    pl.semaphore_wait(
        barrier, NX * NY - 1 + has_down.astype(jnp.int32) + has_up.astype(jnp.int32)
    )
    for k in (OWN, 2, 4, 0, 1, 5, 6, 7):
        spread(k)
    own = pltpu.make_async_copy(slices.at[win, xc], blocks[OWN].at[own_place], in_own)
    own.start()
    p_copies = []
    for step in range(1, NX):
        p_copies.append(
            remote(
                pair_buf.at[my_pairs], pair_buf.at[my_pairs], p_send.at[step], p_recv.at[step],
                row + x_at(step), win,
            )
        )
        p_copies[-1].start()

    def halo_copy(k, side):
        lo, there, to = ((16, 48, down), (32, 0, up))[side]
        return remote(
            blocks[k].at[pl.ds(lo, 16)], blocks[k].at[pl.ds(there, 16)],
            z_send.at[k, side], z_recv.at[k, side], to, win,
        )

    def halo(k):
        for side, there in enumerate((has_down, has_up)):

            @pl.when(there)
            def _():
                halo_copy(k, side).start()

    def halo_wait(k):
        for side, there in enumerate((has_up, has_down)):

            @pl.when(there)
            def _():
                halo_copy(k, side).wait_recv()

    def row_there(k):
        spread_all(k).wait_recv()
        halo(k)

    own.wait()
    for k in (OWN, 2, 4, 0, 1):
        row_there(k)

    for step in range(1, NX):
        frm = lax.rem(xc + NX - step, NX)
        theirs = pl.ds(pl.multiple_of(frm * 8, 8), 8)
        remote(
            pair_buf.at[theirs], pair_buf.at[theirs], p_send.at[step], p_recv.at[step],
            row + frm, win,
        ).wait_recv()
    to_smem = pltpu.make_async_copy(pair_buf, pair_idx, p_own)
    to_smem.start()
    to_smem.wait()

    for k in range(EARLY + 1, NY):
        row_there(k)

    def accumulate(held, y, more):
        def owner(o, carry):
            for q in range(PO // NY):
                j = y * (PO // NY) + q
                a, b = pair_idx[o * 8, j], pair_idx[o * 8 + 1, j]
                first = held[:, a].astype(jnp.float32)
                second = held[:, b].astype(jnp.float32)
                a_re, a_im, b_re, b_im = first[:, :8], first[:, 8:], second[:, :8], second[:, 8:]
                real = jnp.sum(a_re * b_re + a_im * b_im, axis=0)
                imag = jnp.sum(a_re * b_im - a_im * b_re, axis=0)
                at = pl.ds(pl.multiple_of((y * PO + o * 4 + q) * 8, 8), 8)
                if more:
                    real, imag = re_acc[at, :] + real, im_acc[at, :] + imag
                re_acc[at, :] = real
                im_acc[at, :] = imag
            return carry

        lax.fori_loop(0, NX, owner, 0)

    for k in range(EARLY):
        halo_wait(k)

    def first_half(y, carry):
        accumulate(early, y, False)
        return carry

    lax.fori_loop(0, NY, first_half, 0)
    for k in range(EARLY, NY):
        halo_wait(k)

    loads[1 + B_DEV].wait()
    my_rows = pl.ds(pl.multiple_of(me * 8, 8), 8)
    for k in OUT_ORDER:
        y = y_at(k)
        accumulate(late, y, True)
        at = y * (PO * 8)
        cross = jnp.concatenate(
            [
                sum(s[pl.ds(at + seg, NX * 8, stride=SEGS), :] for seg in range(SEGS))
                for s in (re_acc, im_acc)
            ],
            axis=1,
        )
        stacks[y] = jnp.dot(
            cross, inv_buf[...], precision=lax.Precision.HIGHEST, preferred_element_type=jnp.float32
        ).reshape(NX, 8, LAGS)

        def send(to):
            remote(
                stacks.at[y, to], rows_in.at[my_rows], out_send.at[k], out_recv, row + to, y
            ).start()

        each_x(1 if k == OWN else 0, send)
    out_copy = pltpu.make_async_copy(stacks.at[win, xc], rows_in.at[my_rows], out_own)
    out_copy.start()

    for copy in p_copies:
        copy.wait_send()
    for k in range(NY):
        spread_all(k).wait_send()
        many = rows_in.at[pl.ds(0, (NX - 1 if k == OWN else NX) * 8)]
        remote(many, many, out_send.at[k], out_recv, chan, win).wait_send()
        for side, there in enumerate((has_down, has_up)):

            @pl.when(there)
            def _():
                halo_copy(k, side).wait_send()

    out_copy.wait()
    many = rows_in.at[pl.ds(0, (NX * NY - 1) * 8)]
    remote(many, many, out_send.at[0], out_recv, chan, win).wait_recv()


def mask_kernel(low_ref, high_ref, used_ref, v_ref, out_ref):
    lag = lax.broadcasted_iota(jnp.int32, (NX * NY, LAGS), 1)
    start = lax.axis_index("win") * (PO // NY)
    for slot in range(PO // NY):
        here = start + slot
        high = jnp.where(here < used_ref[0], high_ref[here], 0)
        keep = (lag >= low_ref[here]) & (lag < high)
        for c in range(2):
            part = v_ref[pl.ds(slot * 2 + c, NX * NY, stride=8), :]
            out_ref[pl.ds(slot * BLOCK + c, NX * NY, stride=2), :] = jnp.where(keep, part, 0.0)


def masked(lag_low, lag_high, slot_count, rows):
    smem = pl.BlockSpec(memory_space=pltpu.SMEM)
    vmem = pl.BlockSpec(memory_space=pltpu.VMEM)
    share = PO // NY
    return pl.pallas_call(
        mask_kernel,
        out_shape=jax.ShapeDtypeStruct((share * BLOCK, LAGS), jnp.float32),
        in_specs=[smem, smem, smem, vmem],
        out_specs=vmem,
    )(lag_low, lag_high, slot_count, rows).reshape(
        share, BLOCK, LAGS
    )


def per_device(records, block_pairs, lag_low, lag_high, slot_count):
    dma = pltpu.SemaphoreType.DMA
    hbm = pl.BlockSpec(memory_space=pltpu.HBM)
    vmem = pl.BlockSpec(memory_space=pltpu.VMEM)
    near = NY - EARLY
    bf16, f32, i32 = jnp.bfloat16, jnp.float32, jnp.int32
    rows = pl.pallas_call(
        kernel,
        out_shape=jax.ShapeDtypeStruct((NY * NX * 8, LAGS), f32),
        in_specs=[hbm] * 3 + [vmem],
        out_specs=hbm,
        scratch_shapes=[
            pltpu.VMEM((B_DEV, SEGS, BLOCK, NT), bf16),
            pltpu.VMEM((NT, 2 * F), bf16),
            pltpu.VMEM((2 * F, LAGS), f32),
            pltpu.VMEM((SEGS * BLOCK, F), f32),
            pltpu.VMEM((SEGS * BLOCK, F), f32),
            pltpu.VMEM((NY, NX, B_DEV, ROWS, F), bf16),
            pltpu.VMEM((EARLY, NBLK, ROWS, F), bf16),
            pltpu.VMEM((near, NBLK, ROWS, F), bf16),
            pltpu.VMEM((NX * PO * 8, F), f32),
            pltpu.VMEM((NX * PO * 8, F), f32),
            pltpu.VMEM((NX * 8, 128), i32),
            pltpu.SMEM((NX * 8, 128), i32),
            pltpu.VMEM((NY, NX, 8, LAGS), f32),
            dma((B_DEV + 2,)),
            dma((NY,)), dma((NY,)), dma(()),
            dma((NY, 2)), dma((NY, 2)),
            dma((NX,)), dma((NX,)), dma(()),
            dma((NY,)), dma(()), dma(()),
        ],
        compiler_params=pltpu.CompilerParams(
            collective_id=0, has_side_effects=True, vmem_limit_bytes=63 << 20
        ),
    )(
        records, jnp.asarray(forward_table()), jnp.asarray(inverse_table()), block_pairs.T
    )
    return masked(lag_low, lag_high, slot_count, rows)


def solution(mesh):
    in_specs = (P("win", "chan", None), P("chan", None), P("chan"), P("chan"), P("chan"))
    out_specs = P(("chan", "win"), None, None)
    return jax.shard_map(
        per_device, mesh=mesh, in_specs=in_specs, out_specs=out_specs, check_vma=False
    )
```
